32 devices in a mesh: gx: 16 (over z, y, core), ta: 2 (over x).
Axes of the slice: x: 2, y: 2, z: 4, core: 2. Of those that a mesh axis runs over, the one named last changes fastest.
Arguments:
- source: float32 [32, 512, 512], P('ta', 'gx'), may hold values from -6 to 6
- previous: float32 [32, 512, 512], P('ta', 'gx'), may hold values from -6 to 6
- time_modes: float32 [32, 32], replicated, as said below
- time_back: float32 [32, 32], replicated, as said below
- step_code: int32 [32], P('ta'), may hold values from 0 to 32
Outputs:
- next_iterate: float32 [32, 512, 512], P('ta', 'gx')
The draws below stay inside these ranges and needn't reach their ends.
Inputs may be any that keep to these rules, and one draw needn't show every extreme that they name: time_modes times time_back is the identity up to rounding. time_back is the inverse of time_modes up to rounding.
All inputs are finite; a program needn't handle non-finite values.
Results may differ from the reference program's by a relative error of at most 0.0001.
Values sent between devices are 32-bit elements; how exact they have to be, the bound alone decides.
A program may use at most 64 MiB of HBM per device.

```python
import jax
import jax.numpy as jnp
from jax import lax

CX = 32
CY = 64
CZ = 8
CYCLES = 2
LEVELS = 3
NT = 32
NX = 512
ZY = 512
N_GX = 16


def time_pair(key):
    noise_key = jax.random.fold_in(key, 7)
    noise = jax.random.normal(noise_key, (NT, NT), jnp.float32)
    back = jnp.eye(NT, dtype=jnp.float32) + 0.3 * noise / jnp.sqrt(NT * 1.0)
    return (back, jnp.linalg.inv(back))


def draw_time_back(key, part):
    return time_pair(key)[0]


def draw_time_modes(key, part):
    return time_pair(key)[1]


def with_ends(entries, key, least, top_value):
    shape = entries.shape
    spot = [jax.random.randint(jax.random.fold_in(key, axis), (), 0, shape[axis]) for axis in range(len(shape))]
    entries = entries.at[tuple(spot)].set(least)
    longest = shape.index(max(shape))
    spot[longest] = (spot[longest] + 1) % shape[longest]
    return entries.at[tuple(spot)].set(top_value)


def block_levels(key, shape, pieces, low, largest):
    def one(dim, shards_of):
        draws = jax.random.uniform(jax.random.fold_in(jax.random.fold_in(key, 6), dim), (shards_of,), jnp.float32, low / len(pieces), largest / len(pieces))
        return jnp.repeat(jnp.exp(draws), shape[dim] // shards_of).reshape((-1,) + (1,) * (len(shape) - dim - 1))

    factor_of = one(*pieces[0])
    for cut in pieces[1:]:
        factor_of = factor_of * one(*cut)
    return factor_of


def normal_values(rng, extent, deviation, limit, shards=(), kind=jnp.bfloat16):
    loudness = block_levels(rng, extent, shards, -0.22, 0.18) if shards else 1.0
    array = jax.random.normal(rng, extent, jnp.float32) * deviation * loudness
    return jnp.minimum(jnp.maximum(array, -limit), limit).astype(kind)


def setup_inputs(seed: int = 0) -> dict:
    arg_keys = jax.random.split(jax.random.key(seed), 6)
    source = normal_values(arg_keys[0], (NT, NX, ZY), 1.0, 6.0, ((0, 2), (1, 16)), jnp.float32)
    previous = normal_values(arg_keys[1], (NT, NX, ZY), 1.0, 6.0, ((0, 2), (1, 16)), jnp.float32)
    time_modes = draw_time_modes(jax.random.fold_in(arg_keys[5], 71), 0)
    time_back = draw_time_back(jax.random.fold_in(arg_keys[5], 71), 0)
    step_code = with_ends(jax.random.randint(arg_keys[4], (NT,), 0, 33), jax.random.fold_in(arg_keys[4], 1), 0, 32).astype(jnp.int32)
    return {"source": source, "previous": previous, "time_modes": time_modes, "time_back": time_back, "step_code": step_code}


ROBIN = 1.0
DAMPING = 0.8

def neighbour_sum(field, zdim, ydim):
    rank = field.ndim
    xpad = jnp.pad(field, [(0, 0)] * (rank - 2) + [(1, 1), (0, 0)])
    total = xpad[..., 2:, :] + xpad[..., :-2, :]
    zpad = jnp.pad(field, [(0, 0)] * (rank - 1) + [(ydim, ydim)])
    total = total + zpad[..., 2 * ydim:] + zpad[..., :-2 * ydim]
    ypad = jnp.pad(field, [(0, 0)] * (rank - 1) + [(1, 1)])
    column = jnp.arange(zdim * ydim) % ydim
    upper = (column != ydim - 1).astype(jnp.float32)
    lower = (column != 0).astype(jnp.float32)
    return total + upper * ypad[..., 2:] + lower * ypad[..., :-2]

def edge_weights(xdim, left, right):
    position = jnp.arange(xdim)[:, None]
    return left * (position == 0).astype(jnp.float32) + right * (position == xdim - 1).astype(jnp.float32)

def smooth(field, target, diag, scale, zdim, ydim, sweeps):
    for sweep in range(sweeps):
        applied = diag * field - scale * neighbour_sum(field, zdim, ydim)
        field = field + DAMPING * (target - applied) / diag
    return field

def restrict(field, zdim, ydim):
    modes, groups, xdim, plane = field.shape
    blocks = field.reshape(modes, groups, xdim // 2, 2, zdim // 2, 2, ydim // 2, 2)
    return jnp.mean(blocks, axis=(3, 5, 7)).reshape(modes, groups, xdim // 2, zdim // 2 * (ydim // 2))

def prolong(field, zdim, ydim):
    modes, groups, xdim, plane = field.shape
    spread = field.reshape(modes, groups, xdim, 1, zdim // 2, 1, ydim // 2, 1)
    spread = jnp.broadcast_to(spread, (modes, groups, xdim, 2, zdim // 2, 2, ydim // 2, 2))
    return spread.reshape(modes, groups, 2 * xdim, zdim * ydim)

def vcycle(field, target, shifts, left, right, level, zdim, ydim):
    scale = 0.25 ** level
    edge = edge_weights(field.shape[2], left, right)
    diag = shifts + scale * (6.0 + edge)
    if level == LEVELS - 1:
        return smooth(field, target, diag, scale, zdim, ydim, 6)
    field = smooth(field, target, diag, scale, zdim, ydim, 2)
    resid = target - (diag * field - scale * neighbour_sum(field, zdim, ydim))
    coarse_target = restrict(resid, zdim, ydim)
    coarse = vcycle(jnp.zeros_like(coarse_target), coarse_target, shifts, left, right, level + 1, zdim // 2, ydim // 2)
    field = field + prolong(coarse, zdim, ydim)
    return smooth(field, target, diag, scale, zdim, ydim, 2)

def solve_modes(target, shifts, left, right):
    field = jnp.zeros_like(target)
    for cycle in range(CYCLES):
        field = vcycle(field, target, shifts, left, right, 0, CZ, CY)
    return field

def reference(source, previous, time_modes, time_back, step_code):
    steps, cells_x, plane = source.shape
    groups = N_GX
    src = source.reshape(steps, groups, CX, plane)
    prev = previous.reshape(steps, groups, CX, plane)
    index = jnp.arange(groups)
    has_left = (index > 0).astype(jnp.float32)
    has_right = (index < groups - 1).astype(jnp.float32)
    left_near = jnp.pad(prev[:, :-1, -1, :], ((0, 0), (1, 0), (0, 0)))
    right_near = jnp.pad(prev[:, 1:, 0, :], ((0, 0), (0, 1), (0, 0)))
    trace_left = has_left[None, :, None] * (left_near - ROBIN * prev[:, :, 0, :])
    trace_right = has_right[None, :, None] * (right_near - ROBIN * prev[:, :, -1, :])
    rhs = src.at[:, :, 0, :].add(trace_left).at[:, :, -1, :].add(trace_right)
    modes = jnp.einsum('mt,tgxc->mgxc', time_modes, rhs, precision=lax.Precision.HIGHEST)
    shifts = (0.05 * jnp.exp2(step_code.astype(jnp.float32) / 4.0)).reshape(steps, 1, 1, 1)
    left = (ROBIN * has_left).reshape(1, groups, 1, 1)
    right = (ROBIN * has_right).reshape(1, groups, 1, 1)
    solved = solve_modes(modes, shifts, left, right)
    result = jnp.einsum('tm,mgxc->tgxc', time_back, solved, precision=lax.Precision.HIGHEST)
    return result.reshape(steps, cells_x, plane)
```

```python
import functools

import jax
import jax.numpy as jnp
from jax import lax
from jax.experimental import pallas as pl
from jax.experimental.pallas import tpu as pltpu
from jax.sharding import PartitionSpec as P

CY = 64
CZ = 8
CYCLES = 2

ROBIN = 1.0
DAMPING = 0.8

SUB = 8
LANES = 128
PAIRS = SUB // 2
GROUP = LANES // PAIRS
MESH = pl.DeviceIdType.MESH
HIGHEST = lax.Precision.HIGHEST


def spread(matrix, steps):
    wide = jnp.concatenate([matrix] * SUB, axis=1)
    rows = steps * SUB
    tall = jnp.broadcast_to(wide[:, None, :], (steps, SUB, SUB * GROUP)).reshape(rows, SUB * GROUP)
    row = lax.broadcasted_iota(jnp.int32, (rows, SUB * GROUP), 0) % SUB
    lane = lax.broadcasted_iota(jnp.int32, (rows, SUB * GROUP), 1)
    want = (lane % LANES) // GROUP * 2 + lane // LANES
    return jnp.where(row == want, tall, 0.0)


def each(count, action):
    if count == 1:
        action(0)
    else:
        lax.fori_loop(0, count, lambda i, carry: (action(i), carry)[1], 0)


def gather_kernel(
    peers, groups_gx, src, prev, shift, table, f_out, shift_out,
    held, near_left, near_right, first, last, weights,
    send_in, recv_in, send_lo, recv_lo, send_hi, recv_hi, send_sh, recv_sh,
    halo_send, halo_recv, local,
):
    steps, cells_x, plane = src.shape
    chunks = cells_x // SUB
    me = lax.axis_index("ta")
    spot = lax.axis_index("gx")
    has_left = spot > 0
    has_right = spot < groups_gx - 1

    barrier = pltpu.get_barrier_semaphore()
    for d in range(1, peers):
        pl.semaphore_signal(
            barrier, inc=1, device_id={"ta": lax.rem(me + d, peers)}, device_id_type=MESH
        )

    @pl.when(has_left)
    def _():
        pl.semaphore_signal(barrier, inc=1, device_id={"gx": spot - 1}, device_id_type=MESH)

    @pl.when(has_right)
    def _():
        pl.semaphore_signal(barrier, inc=1, device_id={"gx": spot + 1}, device_id_type=MESH)

    own = [
        pltpu.make_async_copy(src, held.at[me], local.at[0]),
        pltpu.make_async_copy(prev.at[:, 0:SUB, :], first, local.at[1]),
        pltpu.make_async_copy(prev.at[:, cells_x - SUB : cells_x, :], last, local.at[2]),
    ]
    for copy in own:
        copy.start()

    sides = has_left.astype(jnp.int32) + has_right.astype(jnp.int32)
    pl.semaphore_wait(barrier, peers - 1 + sides)

    def remote(source, target, send, recv, where):
        return pltpu.make_async_remote_copy(
            src_ref=source, dst_ref=target, send_sem=send, recv_sem=recv,
            device_id=where, device_id_type=MESH,
        )

    to_left = remote(
        prev.at[:, 0:SUB, :], near_right, halo_send.at[0], halo_recv.at[0], {"gx": spot - 1}
    )
    to_right = remote(
        prev.at[:, cells_x - SUB : cells_x, :], near_left, halo_send.at[1], halo_recv.at[1],
        {"gx": spot + 1},
    )

    @pl.when(has_left)
    def _():
        to_left.start()

    @pl.when(has_right)
    def _():
        to_right.start()

    inner = []
    for d in range(1, peers):
        where = {"ta": lax.rem(me + d, peers)}
        inner.append(remote(shift, shift_out.at[me], send_sh.at[d], recv_sh.at[d], where))
        inner.append(
            remote(
                src.at[:, SUB : cells_x - SUB, :],
                held.at[me, :, SUB : cells_x - SUB, :],
                send_in.at[d], recv_in.at[d], where,
            )
        )
    for copy in inner:
        copy.start()
    shift_out[me] = shift[...]

    def weigh(part):
        for block in range(peers):
            rows = table[part, :, block * steps : (block + 1) * steps]
            weights[part, block] = spread(rows.T, steps)

    each(f_out.shape[0], weigh)

    for copy in own:
        copy.wait()

    row = lax.broadcasted_iota(jnp.int32, (steps, SUB, plane), 1)

    @pl.when(has_right)
    def _():
        to_right.wait_send()
        pltpu.make_async_copy(near_right, near_right, halo_recv.at[0]).wait()
        trace = near_right[:, 0:1, :] - ROBIN * last[:, SUB - 1 : SUB, :]
        block = held[me, :, cells_x - SUB : cells_x, :]
        held[me, :, cells_x - SUB : cells_x, :] = block + jnp.where(row == SUB - 1, trace, 0.0)

    @pl.when(has_left)
    def _():
        to_left.wait_send()
        pltpu.make_async_copy(near_left, near_left, halo_recv.at[1]).wait()
        trace = near_left[:, SUB - 1 : SUB, :] - ROBIN * first[:, 0:1, :]
        block = held[me, :, 0:SUB, :]
        held[me, :, 0:SUB, :] = block + jnp.where(row == 0, trace, 0.0)

    def transform(who, chunk, start):
        block = held[who, :, chunk * SUB : (chunk + 1) * SUB, :].reshape(steps * SUB, plane)

        def one(part):
            term = lax.dot_general(
                block, weights[part, who], (((0,), (0,)), ((), ())), precision=HIGHEST,
                preferred_element_type=jnp.float32,
            )
            for half in range(2):
                piece = term[:, half * LANES : (half + 1) * LANES].reshape(f_out.shape[3:])
                if start:
                    f_out[part, chunk, half] = piece
                else:
                    f_out[part, chunk, half] += piece

        each(f_out.shape[0], one)

    for chunk in range(1, chunks - 1):
        transform(me, chunk, True)

    outer = []
    for d in range(1, peers):
        where = {"ta": lax.rem(me + d, peers)}
        outer.append((
            remote(held.at[me, :, 0:SUB, :], held.at[me, :, 0:SUB, :],
                   send_lo.at[d], recv_lo.at[d], where),
            remote(held.at[me, :, cells_x - SUB : cells_x, :],
                   held.at[me, :, cells_x - SUB : cells_x, :],
                   send_hi.at[d], recv_hi.at[d], where),
        ))
    for low, high in outer:
        low.start()
        high.start()

    transform(me, 0, True)
    transform(me, chunks - 1, True)

    for copy in inner:
        copy.wait()
    for d in range(1, peers):
        who = lax.rem(me - d + peers, peers)
        for chunk in range(1, chunks - 1):
            transform(who, chunk, False)
    for d, (low, high) in enumerate(outer, 1):
        who = lax.rem(me - d + peers, peers)
        low.wait()
        transform(who, 0, False)
        high.wait()
        transform(who, chunks - 1, False)


def solve_kernel(peers, groups_gx, f_ref, shift, table, out, va, vb, g1, u1a, u1b, g2, u2a, u2b, fold, fold1, up1, up0):
    parts, chunks, _, zdim, ydim, _ = f_ref.shape
    steps = out.shape[0]
    me = lax.axis_index("ta")
    spot = lax.axis_index("gx")
    left = jnp.where(spot > 0, ROBIN, 0.0).astype(jnp.float32)
    right = jnp.where(spot < groups_gx - 1, ROBIN, 0.0).astype(jnp.float32)
    lane = lax.broadcasted_iota(jnp.int32, (SUB, LANES), 1)
    lane_mode = lane % GROUP
    zero = jnp.zeros((SUB, LANES), jnp.float32)
    z1, y1, z2, y2 = zdim // 2, ydim // 2, zdim // 4, ydim // 4

    def clear(ref, lead, zn, yn):
        def body(z, carry):
            for index in lead:
                ref[index + (z,)] = jnp.zeros((yn + 2 * SUB, LANES), jnp.float32)
            return carry
        for z in (0, zn + 1):
            body(z, 0)

        def edges(z, carry):
            for index in lead:
                ref[index + (z, slice(0, SUB))] = zero
                ref[index + (z, slice(SUB + yn, yn + 2 * SUB))] = zero
            return carry
        lax.fori_loop(1, zn + 1, edges, 0)

    lead0 = [(g, b) for g in range(chunks) for b in range(2)]
    lead1 = [(g,) for g in range(chunks)]
    for ref in (va, vb):
        clear(ref, lead0, zdim, ydim)
    for ref in (u1a, u1b):
        clear(ref, lead1, z1, y1)
    for ref in (u2a, u2b):
        clear(ref, lead1, z2, y2)

    def near(ref, index, z, y):
        base = SUB + y
        return (
            ref[index + (z + 1, slice(base - 1, base - 1 + SUB))]
            + ref[index + (z + 1, slice(base + 1, base + 1 + SUB))]
            + ref[index + (z, slice(base, base + SUB))]
            + ref[index + (z + 2, slice(base, base + SUB))]
        )

    def center(ref, index, z, y):
        return ref[index + (z + 1, slice(SUB + y, 2 * SUB + y))]

    def around0(ref, z, y):
        cur = {i: center(ref, i, z, y) for i in lead0}
        down = [pltpu.roll(cur[g, 1], GROUP, 1) for g in range(chunks)]
        upper = [pltpu.roll(cur[g, 0], LANES - GROUP, 1) for g in range(chunks)]
        total = {}
        for g in range(chunks):
            low = jnp.where(lane < GROUP, down[g - 1] if g else zero, down[g])
            total[g, 0] = near(ref, (g, 0), z, y) + (cur[g, 1] + low)
            high = jnp.where(
                lane >= LANES - GROUP, upper[g + 1] if g < chunks - 1 else zero, upper[g]
            )
            total[g, 1] = near(ref, (g, 1), z, y) + (cur[g, 0] + high)
        return cur, total

    def around1(ref, z, y):
        cur = {i: center(ref, i, z, y) for i in lead1}
        down = [pltpu.roll(cur[g,], GROUP, 1) for g in range(chunks)]
        upper = [pltpu.roll(cur[g,], LANES - GROUP, 1) for g in range(chunks)]
        total = {}
        for g in range(chunks):
            low = jnp.where(lane < GROUP, down[g - 1] if g else zero, down[g])
            high = jnp.where(
                lane >= LANES - GROUP, upper[g + 1] if g < chunks - 1 else zero, upper[g]
            )
            total[g,] = near(ref, (g,), z, y) + (low + high)
        return cur, total

    def around2(ref, z, y):
        cur = {i: center(ref, i, z, y) for i in lead1}
        swap = [pltpu.roll(cur[g,], LANES // 2, 1) for g in range(chunks)]
        total = {}
        for g in range(chunks):
            side = jnp.where(
                lane < LANES // 2, swap[g - 1] if g else zero, swap[g + 1] if g < chunks - 1 else zero
            )
            total[g,] = near(ref, (g,), z, y) + (swap[g] + side)
        return cur, total

    def solve(part):
        width = GROUP // steps
        shifts = shift[part * width]
        for block in range(1, width):
            shifts = jnp.where(lane_mode >= block * steps, shift[part * width + block], shifts)

        def diagonals(scale, size):
            low = jnp.where(lane < size, left, 0.0)
            high = jnp.where(lane >= LANES - size, right, 0.0)
            plain = shifts + scale * 6.0
            return plain, shifts + scale * (6.0 + low), shifts + scale * (6.0 + high)

        d0, d0l, d0r = diagonals(1.0, GROUP)
        d1, d1l, d1r = diagonals(0.25, GROUP)
        d2, d2l, d2r = diagonals(0.0625, LANES // 2)
        diag0 = {i: d0 for i in lead0}
        diag0[0, 0] = d0l
        diag0[chunks - 1, 1] = d0r
        diag1 = {i: d1 for i in lead1}
        diag1[0,] = d1l
        diag1[chunks - 1,] = d1r
        diag2 = {i: d2 for i in lead1}
        diag2[0,] = d2l
        diag2[chunks - 1,] = d2r

        def table_of(diag):
            seen = {}
            out = {}
            for key, value in diag.items():
                if id(value) not in seen:
                    seen[id(value)] = DAMPING / value
                out[key] = seen[id(value)]
            return out

        w0, w1, w2 = table_of(diag0), table_of(diag1), table_of(diag2)

        def target0(i, z, y):
            return f_ref[(part,) + i + (z, slice(y, y + SUB))]

        def start0(dst):
            def body(z, carry):
                for y in range(0, ydim, SUB):
                    for i in lead0:
                        dst[i + (z + 1, slice(SUB + y, 2 * SUB + y))] = w0[i] * target0(i, z, y)
                return carry
            lax.fori_loop(0, zdim, body, 0)

        def sweep0(src, dst):
            def body(z, carry):
                for y in range(0, ydim, SUB):
                    cur, total = around0(src, z, y)
                    for i in lead0:
                        dst[i + (z + 1, slice(SUB + y, 2 * SUB + y))] = (
                            (1.0 - DAMPING) * cur[i] + w0[i] * (target0(i, z, y) + total[i])
                        )
                return carry
            lax.fori_loop(0, zdim, body, 0)

        def restrict0(src):
            def body(zc, carry):
                for y in range(0, ydim, SUB):
                    sums = [None] * chunks
                    for dz in range(2):
                        z = 2 * zc + dz
                        cur, total = around0(src, z, y)
                        for i in lead0:
                            r = target0(i, z, y) - (diag0[i] * cur[i] - total[i])
                            sums[i[0]] = r if sums[i[0]] is None else sums[i[0]] + r
                    for g in range(chunks):
                        fold[g, zc, y : y + SUB] = sums[g]
                for g in range(chunks):
                    g1[g, zc] = 0.125 * (
                        fold[g, zc, pl.ds(0, y1, stride=2), :] + fold[g, zc, pl.ds(1, y1, stride=2), :]
                    )
                return carry
            lax.fori_loop(0, z1, body, 0)

        def add0(ref):
            def body(zc, carry):
                for g in range(chunks):
                    value = center_all(u1a, g, zc, y1)
                    up0[g, zc, pl.ds(0, y1, stride=2), :] = value
                    up0[g, zc, pl.ds(1, y1, stride=2), :] = value
                for g in range(chunks):
                    for y in range(0, ydim, SUB):
                        extra = up0[g, zc, y : y + SUB]
                        for b in range(2):
                            for dz in range(2):
                                at = (g, b, 2 * zc + dz + 1, slice(SUB + y, 2 * SUB + y))
                                ref[at] = ref[at] + extra
                return carry
            lax.fori_loop(0, z1, body, 0)

        def center_all(ref, g, z, yn):
            return ref[g, z + 1, SUB : SUB + yn]

        def start(dst, target, w, zn, yn):
            for z in range(zn):
                for y in range(0, yn, SUB):
                    for i in lead1:
                        dst[i + (z + 1, slice(SUB + y, 2 * SUB + y))] = (
                            w[i] * target[i + (z, slice(y, y + SUB))]
                        )

        def sweep(around, src, dst, target, w, scale, zn, yn):
            for z in range(zn):
                for y in range(0, yn, SUB):
                    cur, total = around(src, z, y)
                    for i in lead1:
                        dst[i + (z + 1, slice(SUB + y, 2 * SUB + y))] = (1.0 - DAMPING) * cur[i] + w[
                            i
                        ] * (target[i + (z, slice(y, y + SUB))] + scale * total[i])

        def restrict1(src):
            for zc in range(z2):
                for y in range(0, y1, SUB):
                    sums = [None] * chunks
                    for dz in range(2):
                        z = 2 * zc + dz
                        cur, total = around1(src, z, y)
                        for i in lead1:
                            r = g1[i + (z, slice(y, y + SUB))] - (
                                diag1[i] * cur[i] - 0.25 * total[i]
                            )
                            sums[i[0]] = r if sums[i[0]] is None else sums[i[0]] + r
                    for g in range(chunks):
                        even = (lane // GROUP) % 2 == 0
                        other = jnp.where(
                            even,
                            pltpu.roll(sums[g], LANES - GROUP, 1),
                            pltpu.roll(sums[g], GROUP, 1),
                        )
                        fold1[g, zc, y : y + SUB] = sums[g] + other
                for g in range(chunks):
                    g2[g, zc] = 0.125 * (
                        fold1[g, zc, pl.ds(0, y2, stride=2), :] + fold1[g, zc, pl.ds(1, y2, stride=2), :]
                    )

        def add1(ref):
            for zc in range(z2):
                for g in range(chunks):
                    value = center_all(u2b, g, zc, y2)
                    up1[g, zc, pl.ds(0, y2, stride=2), :] = value
                    up1[g, zc, pl.ds(1, y2, stride=2), :] = value
                for g in range(chunks):
                    for y in range(0, y1, SUB):
                        extra = up1[g, zc, y : y + SUB]
                        for dz in range(2):
                            at = (g, 2 * zc + dz + 1, slice(SUB + y, 2 * SUB + y))
                            ref[at] = ref[at] + extra

        for cycle in range(CYCLES):
            if cycle == 0:
                start0(va)
            else:
                sweep0(vb, va)
            sweep0(va, vb)
            restrict0(vb)
            start(u1a, g1, w1, z1, y1)
            sweep(around1, u1a, u1b, g1, w1, 0.25, z1, y1)
            restrict1(u1b)
            start(u2a, g2, w2, z2, y2)
            here, there = u2a, u2b
            for _ in range(5):
                sweep(around2, here, there, g2, w2, 0.0625, z2, y2)
                here, there = there, here
            add1(u1b)
            sweep(around1, u1b, u1a, g1, w1, 0.25, z1, y1)
            sweep(around1, u1a, u1b, g1, w1, 0.25, z1, y1)
            for g in range(chunks):
                for z in range(z1):
                    u1a[g, z + 1, SUB : SUB + y1] = u1b[g, z + 1, SUB : SUB + y1]
            add0(vb)
            sweep0(vb, va)
            sweep0(va, vb)

        rows = pl.ds(pl.multiple_of(me * steps, steps), steps)
        weights = spread(table[part, rows], steps)
        for g in range(chunks):
            field = jnp.concatenate(
                [
                    vb[g, b, 1 : zdim + 1, SUB : SUB + ydim].reshape(zdim * ydim, LANES)
                    for b in range(2)
                ],
                axis=1,
            )
            term = lax.dot_general(
                weights, field, (((1,), (1,)), ((), ())), precision=HIGHEST,
                preferred_element_type=jnp.float32,
            ).reshape(steps, SUB, zdim * ydim)
            if parts > 1:
                out[:, g * SUB : (g + 1) * SUB, :] += term
            else:
                out[:, g * SUB : (g + 1) * SUB, :] = term

    if parts > 1:
        out[...] = jnp.zeros_like(out)
    each(parts, solve)


def body(mesh, source, previous, time_modes, time_back, step_code):
    steps, cells_x, plane = source.shape
    total = time_modes.shape[0]
    peers, groups_gx = mesh.shape["ta"], mesh.shape["gx"]
    chunks, parts = cells_x // SUB, total // GROUP
    shifts = 0.05 * jnp.exp2(step_code.astype(jnp.float32) / 4.0)
    shifts = jnp.broadcast_to(jnp.tile(shifts, LANES // steps)[None], (SUB, LANES))
    vmem = pl.BlockSpec(memory_space=pltpu.VMEM)
    anywhere = pl.BlockSpec(memory_space=pl.ANY)
    dma = pltpu.SemaphoreType.DMA
    f32 = jnp.float32
    field = (parts, chunks, 2, CZ, CY, LANES)
    target, every = pl.pallas_call(
        functools.partial(gather_kernel, peers, groups_gx),
        out_shape=(
            jax.ShapeDtypeStruct(field, f32),
            jax.ShapeDtypeStruct((peers, SUB, LANES), f32),
        ),
        in_specs=[anywhere, anywhere, vmem, vmem],
        out_specs=(vmem, vmem),
        scratch_shapes=[
            pltpu.VMEM((peers, steps, cells_x, plane), f32),
            pltpu.VMEM((steps, SUB, plane), f32),
            pltpu.VMEM((steps, SUB, plane), f32),
            pltpu.VMEM((steps, SUB, plane), f32),
            pltpu.VMEM((steps, SUB, plane), f32),
            pltpu.VMEM((parts, peers, steps * SUB, SUB * GROUP), f32),
        ] + [dma((peers,))] * 8 + [dma((2,)), dma((2,)), dma((3,))],
        compiler_params=pltpu.CompilerParams(
            collective_id=0, has_side_effects=True, vmem_limit_bytes=48 << 20
        ),
        name="gather",
    )(source, previous, shifts, time_modes.reshape(parts, GROUP, total))
    wide0 = (chunks, 2, CZ + 2, CY + 2 * SUB, LANES)
    wide1 = (chunks, CZ // 2 + 2, CY // 2 + 2 * SUB, LANES)
    wide2 = (chunks, CZ // 4 + 2, CY // 4 + 2 * SUB, LANES)
    slim1 = (chunks, CZ // 2, CY // 2, LANES)
    slim2 = (chunks, CZ // 4, CY // 4, LANES)
    up0 = (chunks, CZ // 2, CY, LANES)
    up1 = (chunks, CZ // 4, CY // 2, LANES)
    shapes = [wide0, wide0, slim1, wide1, wide1, slim2, wide2, wide2, up0, up1, up1, up0]
    return pl.pallas_call(
        functools.partial(solve_kernel, peers, groups_gx),
        out_shape=jax.ShapeDtypeStruct(source.shape, f32),
        in_specs=[vmem] * 3,
        out_specs=vmem,
        scratch_shapes=[pltpu.VMEM(shape, f32) for shape in shapes],
        compiler_params=pltpu.CompilerParams(vmem_limit_bytes=48 << 20),
        name="solve",
    )(target, every, time_back.reshape(total, parts, GROUP).swapaxes(0, 1))


def solution(mesh):
    placed = (P("ta", "gx", None), P("ta", "gx", None), P(), P(), P("ta"))
    return jax.shard_map(
        functools.partial(body, mesh), mesh=mesh, in_specs=placed,
        out_specs=P("ta", "gx", None), check_vma=False,
    )
```

```python
import functools

import jax
import jax.numpy as jnp
from jax import lax
from jax.experimental import pallas as pl
from jax.experimental.pallas import tpu as pltpu
from jax.sharding import PartitionSpec as P

CY = 64
CZ = 8
CYCLES = 2

ROBIN = 1.0
DAMPING = 0.8

SUB = 8
LANES = 128
PAIRS = SUB // 2
GROUP = LANES // PAIRS
MESH = pl.DeviceIdType.MESH
HIGHEST = lax.Precision.HIGHEST


def spread(matrix, steps):
    wide = jnp.concatenate([matrix] * SUB, axis=1)
    rows = steps * SUB
    tall = jnp.broadcast_to(wide[:, None, :], (steps, SUB, SUB * GROUP)).reshape(rows, SUB * GROUP)
    row = lax.broadcasted_iota(jnp.int32, (rows, SUB * GROUP), 0) % SUB
    lane = lax.broadcasted_iota(jnp.int32, (rows, SUB * GROUP), 1)
    want = (lane % LANES) // GROUP * 2 + lane // LANES
    return jnp.where(row == want, tall, 0.0)


def each(count, action):
    if count == 1:
        action(0)
    else:
        lax.fori_loop(0, count, lambda i, carry: (action(i), carry)[1], 0)


def gather_kernel(
    peers, groups_gx, src, prev, shift, table, f_out, shift_out,
    held, near_left, near_right, first, last, weights,
    send_in, recv_in, send_lo, recv_lo, send_hi, recv_hi, send_sh, recv_sh,
    halo_send, halo_recv, local,
):
    steps, cells_x, plane = src.shape
    chunks = cells_x // SUB
    me = lax.axis_index("ta")
    spot = lax.axis_index("gx")
    has_left = spot > 0
    has_right = spot < groups_gx - 1

    barrier = pltpu.get_barrier_semaphore()
    for d in range(1, peers):
        pl.semaphore_signal(
            barrier, inc=1, device_id={"ta": lax.rem(me + d, peers)}, device_id_type=MESH
        )

    @pl.when(has_left)
    def _():
        pl.semaphore_signal(barrier, inc=1, device_id={"gx": spot - 1}, device_id_type=MESH)

    @pl.when(has_right)
    def _():
        pl.semaphore_signal(barrier, inc=1, device_id={"gx": spot + 1}, device_id_type=MESH)

    own = [
        pltpu.make_async_copy(src, held.at[me], local.at[0]),
        pltpu.make_async_copy(prev.at[:, 0:SUB, :], first, local.at[1]),
        pltpu.make_async_copy(prev.at[:, cells_x - SUB : cells_x, :], last, local.at[2]),
    ]
    for copy in own:
        copy.start()

    sides = has_left.astype(jnp.int32) + has_right.astype(jnp.int32)
    pl.semaphore_wait(barrier, peers - 1 + sides)

    def remote(source, target, send, recv, where):
        return pltpu.make_async_remote_copy(
            src_ref=source, dst_ref=target, send_sem=send, recv_sem=recv,
            device_id=where, device_id_type=MESH,
        )

    to_left = remote(
        prev.at[:, 0:SUB, :], near_right, halo_send.at[0], halo_recv.at[0], {"gx": spot - 1}
    )
    to_right = remote(
        prev.at[:, cells_x - SUB : cells_x, :], near_left, halo_send.at[1], halo_recv.at[1],
        {"gx": spot + 1},
    )

    @pl.when(has_left)
    def _():
        to_left.start()

    @pl.when(has_right)
    def _():
        to_right.start()

    inner = []
    for d in range(1, peers):
        where = {"ta": lax.rem(me + d, peers)}
        inner.append(remote(shift, shift_out.at[me], send_sh.at[d], recv_sh.at[d], where))
        inner.append(
            remote(
                src.at[:, SUB : cells_x - SUB, :],
                held.at[me, :, SUB : cells_x - SUB, :],
                send_in.at[d], recv_in.at[d], where,
            )
        )
    for copy in inner:
        copy.start()
    shift_out[me] = shift[...]

    def weigh(part):
        for block in range(peers):
            rows = table[part, :, block * steps : (block + 1) * steps]
            weights[part, block] = spread(rows.T, steps)

    each(f_out.shape[0], weigh)

    for copy in own:
        copy.wait()

    row = lax.broadcasted_iota(jnp.int32, (steps, SUB, plane), 1)

    @pl.when(has_right)
    def _():
        to_right.wait_send()
        pltpu.make_async_copy(near_right, near_right, halo_recv.at[0]).wait()
        trace = near_right[:, 0:1, :] - ROBIN * last[:, SUB - 1 : SUB, :]
        block = held[me, :, cells_x - SUB : cells_x, :]
        held[me, :, cells_x - SUB : cells_x, :] = block + jnp.where(row == SUB - 1, trace, 0.0)

    @pl.when(has_left)
    def _():
        to_left.wait_send()
        pltpu.make_async_copy(near_left, near_left, halo_recv.at[1]).wait()
        trace = near_left[:, SUB - 1 : SUB, :] - ROBIN * first[:, 0:1, :]
        block = held[me, :, 0:SUB, :]
        held[me, :, 0:SUB, :] = block + jnp.where(row == 0, trace, 0.0)

    def transform(who, chunk, start):
        block = held[who, :, chunk * SUB : (chunk + 1) * SUB, :].reshape(steps * SUB, plane)

        def one(part):
            term = lax.dot_general(
                block, weights[part, who], (((0,), (0,)), ((), ())), precision=HIGHEST,
                preferred_element_type=jnp.float32,
            )
            for half in range(2):
                piece = term[:, half * LANES : (half + 1) * LANES].reshape(f_out.shape[3:])
                if start:
                    f_out[part, chunk, half] = piece
                else:
                    f_out[part, chunk, half] += piece

        each(f_out.shape[0], one)

    for chunk in range(1, chunks - 1):
        transform(me, chunk, True)

    outer = []
    for d in range(1, peers):
        where = {"ta": lax.rem(me + d, peers)}
        outer.append((
            remote(held.at[me, :, 0:SUB, :], held.at[me, :, 0:SUB, :],
                   send_lo.at[d], recv_lo.at[d], where),
            remote(held.at[me, :, cells_x - SUB : cells_x, :],
                   held.at[me, :, cells_x - SUB : cells_x, :],
                   send_hi.at[d], recv_hi.at[d], where),
        ))
    for low, high in outer:
        low.start()
        high.start()

    transform(me, 0, True)
    transform(me, chunks - 1, True)

    for copy in inner:
        copy.wait()
    for d in range(1, peers):
        who = lax.rem(me - d + peers, peers)
        for chunk in range(1, chunks - 1):
            transform(who, chunk, False)
    for d, (low, high) in enumerate(outer, 1):
        who = lax.rem(me - d + peers, peers)
        low.wait()
        transform(who, 0, False)
        high.wait()
        transform(who, chunks - 1, False)


def solve_kernel(peers, groups_gx, f_ref, shift, table, out, va, vb, g1, u1a, u1b, g2, u2a, u2b, fold, fold1, up1, up0):
    parts, chunks, _, zdim, ydim, _ = f_ref.shape
    steps = out.shape[0]
    me = lax.axis_index("ta")
    spot = lax.axis_index("gx")
    left = jnp.where(spot > 0, ROBIN, 0.0).astype(jnp.float32)
    right = jnp.where(spot < groups_gx - 1, ROBIN, 0.0).astype(jnp.float32)
    lane = lax.broadcasted_iota(jnp.int32, (SUB, LANES), 1)
    lane_mode = lane % GROUP
    zero = jnp.zeros((SUB, LANES), jnp.float32)
    z1, y1, z2, y2 = zdim // 2, ydim // 2, zdim // 4, ydim // 4

    def clear(ref, lead, zn, yn):
        def body(z, carry):
            for index in lead:
                ref[index + (z,)] = jnp.zeros((yn + 2 * SUB, LANES), jnp.float32)
            return carry
        for z in (0, zn + 1):
            body(z, 0)

        def edges(z, carry):
            for index in lead:
                ref[index + (z, slice(0, SUB))] = zero
                ref[index + (z, slice(SUB + yn, yn + 2 * SUB))] = zero
            return carry
        lax.fori_loop(1, zn + 1, edges, 0)

    lead0 = [(g, b) for g in range(chunks) for b in range(2)]
    lead1 = [(g,) for g in range(chunks)]
    for ref in (va, vb):
        clear(ref, lead0, zdim, ydim)
    for ref in (u1a, u1b):
        clear(ref, lead1, z1, y1)
    for ref in (u2a, u2b):
        clear(ref, lead1, z2, y2)

    def near(ref, index, z, y):
        base = SUB + y
        return (
            ref[index + (z + 1, slice(base - 1, base - 1 + SUB))]
            + ref[index + (z + 1, slice(base + 1, base + 1 + SUB))]
            + ref[index + (z, slice(base, base + SUB))]
            + ref[index + (z + 2, slice(base, base + SUB))]
        )

    def center(ref, index, z, y):
        return ref[index + (z + 1, slice(SUB + y, 2 * SUB + y))]

    def around0(ref, z, y):
        cur = {i: center(ref, i, z, y) for i in lead0}
        down = [pltpu.roll(cur[g, 1], GROUP, 1) for g in range(chunks)]
        upper = [pltpu.roll(cur[g, 0], LANES - GROUP, 1) for g in range(chunks)]
        total = {}
        for g in range(chunks):
            low = jnp.where(lane < GROUP, down[g - 1] if g else zero, down[g])
            total[g, 0] = near(ref, (g, 0), z, y) + (cur[g, 1] + low)
            high = jnp.where(
                lane >= LANES - GROUP, upper[g + 1] if g < chunks - 1 else zero, upper[g]
            )
            total[g, 1] = near(ref, (g, 1), z, y) + (cur[g, 0] + high)
        return cur, total

    def around1(ref, z, y):
        cur = {i: center(ref, i, z, y) for i in lead1}
        down = [pltpu.roll(cur[g,], GROUP, 1) for g in range(chunks)]
        upper = [pltpu.roll(cur[g,], LANES - GROUP, 1) for g in range(chunks)]
        total = {}
        for g in range(chunks):
            low = jnp.where(lane < GROUP, down[g - 1] if g else zero, down[g])
            high = jnp.where(
                lane >= LANES - GROUP, upper[g + 1] if g < chunks - 1 else zero, upper[g]
            )
            total[g,] = near(ref, (g,), z, y) + (low + high)
        return cur, total

    def around2(ref, z, y):
        cur = {i: center(ref, i, z, y) for i in lead1}
        swap = [pltpu.roll(cur[g,], LANES // 2, 1) for g in range(chunks)]
        total = {}
        for g in range(chunks):
            side = jnp.where(
                lane < LANES // 2, swap[g - 1] if g else zero, swap[g + 1] if g < chunks - 1 else zero
            )
            total[g,] = near(ref, (g,), z, y) + (swap[g] + side)
        return cur, total

    def solve(part):
        width = GROUP // steps
        shifts = shift[part * width]
        for block in range(1, width):
            shifts = jnp.where(lane_mode >= block * steps, shift[part * width + block], shifts)

        def diagonals(scale, size):
            low = jnp.where(lane < size, left, 0.0)
            high = jnp.where(lane >= LANES - size, right, 0.0)
            plain = shifts + scale * 6.0
            return plain, shifts + scale * (6.0 + low), shifts + scale * (6.0 + high)

        d0, d0l, d0r = diagonals(1.0, GROUP)
        d1, d1l, d1r = diagonals(0.25, GROUP)
        d2, d2l, d2r = diagonals(0.0625, LANES // 2)
        diag0 = {i: d0 for i in lead0}
        diag0[0, 0] = d0l
        diag0[chunks - 1, 1] = d0r
        diag1 = {i: d1 for i in lead1}
        diag1[0,] = d1l
        diag1[chunks - 1,] = d1r
        diag2 = {i: d2 for i in lead1}
        diag2[0,] = d2l
        diag2[chunks - 1,] = d2r

        def table_of(diag):
            seen = {}
            out = {}
            for key, value in diag.items():
                if id(value) not in seen:
                    seen[id(value)] = DAMPING / value
                out[key] = seen[id(value)]
            return out

        w0, w1, w2 = table_of(diag0), table_of(diag1), table_of(diag2)

        def target0(i, z, y):
            return f_ref[(part,) + i + (z, slice(y, y + SUB))]

        def start0(dst):
            def body(z, carry):
                for y in range(0, ydim, SUB):
                    for i in lead0:
                        dst[i + (z + 1, slice(SUB + y, 2 * SUB + y))] = w0[i] * target0(i, z, y)
                return carry
            lax.fori_loop(0, zdim, body, 0)

        def sweep0(src, dst):
            def body(z, carry):
                for y in range(0, ydim, SUB):
                    cur, total = around0(src, z, y)
                    for i in lead0:
                        dst[i + (z + 1, slice(SUB + y, 2 * SUB + y))] = (
                            (1.0 - DAMPING) * cur[i] + w0[i] * (target0(i, z, y) + total[i])
                        )
                return carry
            lax.fori_loop(0, zdim, body, 0)

        def restrict0(src):
            def body(zc, carry):
                for y in range(0, ydim, SUB):
                    sums = [None] * chunks
                    for dz in range(2):
                        z = 2 * zc + dz
                        cur, total = around0(src, z, y)
                        for i in lead0:
                            r = target0(i, z, y) - (diag0[i] * cur[i] - total[i])
                            sums[i[0]] = r if sums[i[0]] is None else sums[i[0]] + r
                    for g in range(chunks):
                        fold[g, zc, y : y + SUB] = sums[g]
                for g in range(chunks):
                    g1[g, zc] = 0.125 * (
                        fold[g, zc, pl.ds(0, y1, stride=2), :] + fold[g, zc, pl.ds(1, y1, stride=2), :]
                    )
                return carry
            lax.fori_loop(0, z1, body, 0)

        def add0(ref):
            def body(zc, carry):
                for g in range(chunks):
                    value = center_all(u1b, g, zc, y1)
                    up0[g, zc, pl.ds(0, y1, stride=2), :] = value
                    up0[g, zc, pl.ds(1, y1, stride=2), :] = value
                for g in range(chunks):
                    for y in range(0, ydim, SUB):
                        extra = up0[g, zc, y : y + SUB]
                        for b in range(2):
                            for dz in range(2):
                                at = (g, b, 2 * zc + dz + 1, slice(SUB + y, 2 * SUB + y))
                                ref[at] = ref[at] + extra
                return carry
            lax.fori_loop(0, z1, body, 0)

        def center_all(ref, g, z, yn):
            return ref[g, z + 1, SUB : SUB + yn]

        def start(dst, target, w, zn, yn):
            for z in range(zn):
                for y in range(0, yn, SUB):
                    for i in lead1:
                        dst[i + (z + 1, slice(SUB + y, 2 * SUB + y))] = (
                            w[i] * target[i + (z, slice(y, y + SUB))]
                        )

        def sweep(around, src, dst, target, w, scale, zn, yn):
            for z in range(zn):
                for y in range(0, yn, SUB):
                    cur, total = around(src, z, y)
                    for i in lead1:
                        dst[i + (z + 1, slice(SUB + y, 2 * SUB + y))] = (1.0 - DAMPING) * cur[i] + w[
                            i
                        ] * (target[i + (z, slice(y, y + SUB))] + scale * total[i])

        def restrict1(src):
            for zc in range(z2):
                for y in range(0, y1, SUB):
                    sums = [None] * chunks
                    for dz in range(2):
                        z = 2 * zc + dz
                        cur, total = around1(src, z, y)
                        for i in lead1:
                            r = g1[i + (z, slice(y, y + SUB))] - (
                                diag1[i] * cur[i] - 0.25 * total[i]
                            )
                            sums[i[0]] = r if sums[i[0]] is None else sums[i[0]] + r
                    for g in range(chunks):
                        even = (lane // GROUP) % 2 == 0
                        other = jnp.where(
                            even,
                            pltpu.roll(sums[g], LANES - GROUP, 1),
                            pltpu.roll(sums[g], GROUP, 1),
                        )
                        fold1[g, zc, y : y + SUB] = sums[g] + other
                for g in range(chunks):
                    g2[g, zc] = 0.125 * (
                        fold1[g, zc, pl.ds(0, y2, stride=2), :] + fold1[g, zc, pl.ds(1, y2, stride=2), :]
                    )

        def add1(ref):
            for zc in range(z2):
                for g in range(chunks):
                    value = center_all(u2b, g, zc, y2)
                    up1[g, zc, pl.ds(0, y2, stride=2), :] = value
                    up1[g, zc, pl.ds(1, y2, stride=2), :] = value
                for g in range(chunks):
                    for y in range(0, y1, SUB):
                        extra = up1[g, zc, y : y + SUB]
                        for dz in range(2):
                            at = (g, 2 * zc + dz + 1, slice(SUB + y, 2 * SUB + y))
                            ref[at] = ref[at] + extra

        for cycle in range(CYCLES):
            if cycle == 0:
                start0(va)
            else:
                sweep0(vb, va)
            sweep0(va, vb)
            restrict0(vb)
            start(u1a, g1, w1, z1, y1)
            sweep(around1, u1a, u1b, g1, w1, 0.25, z1, y1)
            restrict1(u1b)
            start(u2a, g2, w2, z2, y2)
            here, there = u2a, u2b
            for _ in range(5):
                sweep(around2, here, there, g2, w2, 0.0625, z2, y2)
                here, there = there, here
            add1(u1b)
            sweep(around1, u1b, u1a, g1, w1, 0.25, z1, y1)
            sweep(around1, u1a, u1b, g1, w1, 0.25, z1, y1)
            add0(vb)
            sweep0(vb, va)
            sweep0(va, vb)

        rows = pl.ds(pl.multiple_of(me * steps, steps), steps)
        weights = spread(table[part, rows], steps)
        for g in range(chunks):
            field = jnp.concatenate(
                [
                    vb[g, b, 1 : zdim + 1, SUB : SUB + ydim].reshape(zdim * ydim, LANES)
                    for b in range(2)
                ],
                axis=1,
            )
            term = lax.dot_general(
                weights, field, (((1,), (1,)), ((), ())), precision=HIGHEST,
                preferred_element_type=jnp.float32,
            ).reshape(steps, SUB, zdim * ydim)
            if parts > 1:
                out[:, g * SUB : (g + 1) * SUB, :] += term
            else:
                out[:, g * SUB : (g + 1) * SUB, :] = term

    if parts > 1:
        out[...] = jnp.zeros_like(out)
    each(parts, solve)


def body(mesh, source, previous, time_modes, time_back, step_code):
    steps, cells_x, plane = source.shape
    total = time_modes.shape[0]
    peers, groups_gx = mesh.shape["ta"], mesh.shape["gx"]
    chunks, parts = cells_x // SUB, total // GROUP
    shifts = 0.05 * jnp.exp2(step_code.astype(jnp.float32) / 4.0)
    shifts = jnp.broadcast_to(jnp.tile(shifts, LANES // steps)[None], (SUB, LANES))
    vmem = pl.BlockSpec(memory_space=pltpu.VMEM)
    anywhere = pl.BlockSpec(memory_space=pltpu.HBM)
    dma = pltpu.SemaphoreType.DMA
    f32 = jnp.float32
    field = (parts, chunks, 2, CZ, CY, LANES)
    target, every = pl.pallas_call(
        functools.partial(gather_kernel, peers, groups_gx),
        out_shape=(
            jax.ShapeDtypeStruct(field, f32),
            jax.ShapeDtypeStruct((peers, SUB, LANES), f32),
        ),
        in_specs=[anywhere, anywhere, vmem, vmem],
        out_specs=(vmem, vmem),
        scratch_shapes=[
            pltpu.VMEM((peers, steps, cells_x, plane), f32),
            pltpu.VMEM((steps, SUB, plane), f32),
            pltpu.VMEM((steps, SUB, plane), f32),
            pltpu.VMEM((steps, SUB, plane), f32),
            pltpu.VMEM((steps, SUB, plane), f32),
            pltpu.VMEM((parts, peers, steps * SUB, SUB * GROUP), f32),
        ] + [dma((peers,))] * 8 + [dma((2,)), dma((2,)), dma((3,))],
        compiler_params=pltpu.CompilerParams(
            collective_id=0, has_side_effects=True, vmem_limit_bytes=60 << 20
        ),
        name="gather",
    )(source, previous, shifts, time_modes.reshape(parts, GROUP, total))
    wide0 = (chunks, 2, CZ + 2, CY + 2 * SUB, LANES)
    wide1 = (chunks, CZ // 2 + 2, CY // 2 + 2 * SUB, LANES)
    wide2 = (chunks, CZ // 4 + 2, CY // 4 + 2 * SUB, LANES)
    slim1 = (chunks, CZ // 2, CY // 2, LANES)
    slim2 = (chunks, CZ // 4, CY // 4, LANES)
    up0 = (chunks, CZ // 2, CY, LANES)
    up1 = (chunks, CZ // 4, CY // 2, LANES)
    shapes = [wide0, wide0, slim1, wide1, wide1, slim2, wide2, wide2, up0, up1, up1, up0]
    return pl.pallas_call(
        functools.partial(solve_kernel, peers, groups_gx),
        out_shape=jax.ShapeDtypeStruct(source.shape, f32),
        in_specs=[vmem] * 3,
        out_specs=vmem,
        scratch_shapes=[pltpu.VMEM(shape, f32) for shape in shapes],
        compiler_params=pltpu.CompilerParams(vmem_limit_bytes=48 << 20),
        name="solve",
    )(target, every, time_back.reshape(total, parts, GROUP).swapaxes(0, 1))


def solution(mesh):
    placed = (P("ta", "gx", None), P("ta", "gx", None), P(), P(), P("ta"))
    return jax.shard_map(
        functools.partial(body, mesh), mesh=mesh, in_specs=placed,
        out_specs=P("ta", "gx", None), check_vma=False,
    )
```
